32 devices in a mesh: band: 2 (over x), row: 16 (over z, y, core).
Axes of the slice: x: 2, y: 2, z: 4, core: 2. Of those that a mesh axis runs over, the one named last changes fastest.
Arguments:
- spectra: float32 [2, 16, 4096, 256], P(None, None, 'row', 'band'), parts along dimension 3, may hold values from -6 to 6
- coda_bins: int32 [8], P('band'), parts along dimension 0, may hold values from 0 to 15
- source_mask: int32 [128, 64], P('band'), parts along dimension 0, may hold values 0 or 1
Outputs:
- third_order: float32 [8192, 2, 4, 128], P(('band', 'row')), parts along dimension 0
The draws below stay inside these ranges and needn't reach their ends.
There are 2 independent parts, one for each index of `band`. The reference program is written for one: setup_inputs(seed, part) draws one part's arguments, and reference() takes and returns one part's arrays. A program takes and returns all parts, laid end to end along the dimension named above; each array names one. Nothing has to cross between parts.
Inputs may be any that keep to these rules, and one draw needn't show every extreme that they name: `coda_bins`: each entry is a bin of the band's spectrum; entries may repeat.
All inputs are finite; a program needn't handle non-finite values.
Results may differ from the reference program's by a relative error of at most 0.004.
Values may be sent and summed in bfloat16 or wider, within the bound.
No kernel may reach another device: no remote copies, remote signals or barrier semaphores. Data moves between devices by JAX's collectives and lax.ppermute only.
A program may use at most 128 MiB of HBM per device.

```python
import jax
import jax.numpy as jnp
from jax import lax

NCH = 4096
NB = 16
F = 4
GRP = 64
W = 128
STRIDE = 32
NG = 64


def touch_ends(entries, own_key, smallest, largest):
    spot = [jax.random.randint(jax.random.fold_in(own_key, axis), (), 0, length) for axis, length in enumerate(entries.shape)]
    widest = entries.shape.index(max(entries.shape))
    beside = spot[:widest] + [(spot[widest] + 1) % entries.shape[widest]] + spot[widest + 1:]
    return entries.at[tuple(spot)].set(smallest).at[tuple(beside)].set(largest)


def block_scale(stream_key, extent, cuts, smallest, high):
    loudness, own = 1.0, jax.random.fold_in(stream_key, 6)
    for axis_at, blocks in cuts:
        steps = jnp.exp(jax.random.uniform(jax.random.fold_in(own, axis_at), (blocks,), jnp.float32, smallest / len(cuts), high / len(cuts)))
        loudness = loudness * jnp.repeat(steps, extent[axis_at] // blocks).reshape([-1 if axis == axis_at else 1 for axis in range(len(extent))])
    return loudness


def normal_values(stream_key, dims, spread, reach, pieces=(), kind=jnp.bfloat16):
    result = jax.random.normal(stream_key, dims, jnp.float32) * spread
    if len(pieces) > 0:
        result = block_scale(stream_key, dims, pieces, -0.22, 0.18) * result
    return jnp.clip(result, min=-reach, max=reach).astype(kind)


def setup_inputs(seed: int = 0, part: int = 0) -> dict:
    streams_of = jax.random.split(jax.random.key(seed), 4)
    part_splits = jax.random.split(jax.random.fold_in(streams_of[3], part), 4)
    spectra = normal_values(part_splits[0], (2, NB, NCH, W), 1.0, 6.0, ((2, 16),), jnp.float32)
    coda_bins = touch_ends(jax.random.randint(part_splits[1], (F,), 0, NB), jax.random.fold_in(part_splits[1], 1), 0, NB - 1).astype(jnp.int32)
    source_mask = touch_ends((jax.random.randint(part_splits[2], (NG, NG), 0, 2) < 1).astype(jnp.int32), jax.random.fold_in(part_splits[2], 1), 0, 1)
    return dict(spectra=spectra, coda_bins=coda_bins, source_mask=source_mask)


def whiten(spectra, coda_bins):
    onehot = (jnp.arange(spectra.shape[1], dtype=jnp.int32)[:, None] == coda_bins[None, :]).astype(jnp.float32)
    picked = jnp.einsum('cbnw,bf->cfwn', spectra, onehot, precision=lax.Precision.HIGHEST)
    power = lax.optimization_barrier(jnp.mean(picked[0] * picked[0] + picked[1] * picked[1], axis=1))
    return (picked / jnp.sqrt(power + 1e-06)[None, :, None, :]).astype(jnp.bfloat16)

def correlate(left_white, right_white):
    left_value = left_white.astype(jnp.float32)
    right_value = right_white.astype(jnp.float32)
    highest = lax.Precision.HIGHEST
    real_part = jnp.einsum('fwa,fwb->fab', left_value[0], right_value[0], precision=highest) + jnp.einsum('fwa,fwb->fab', left_value[1], right_value[1], precision=highest)
    imag_part = jnp.einsum('fwa,fwb->fab', left_value[1], right_value[0], precision=highest) - jnp.einsum('fwa,fwb->fab', left_value[0], right_value[1], precision=highest)
    return jnp.stack([real_part, imag_part]) / left_white.shape[2]

def mask_weights(source_mask, row_ids, col_ids):
    groups = jnp.arange(source_mask.shape[0], dtype=jnp.int32)
    row_onehot = ((row_ids // GRP)[:, None] == groups[None, :]).astype(jnp.float32)
    col_onehot = ((col_ids // GRP)[:, None] == groups[None, :]).astype(jnp.float32)
    table = source_mask.astype(jnp.float32)
    highest = lax.Precision.HIGHEST
    return jnp.dot(jnp.dot(row_onehot, table, precision=highest), col_onehot.T, precision=highest)

def third(left_corr, right_corr):
    highest = lax.Precision.HIGHEST
    real_part = jnp.einsum('fak,ftk->aft', left_corr[0], right_corr[0], precision=highest) + jnp.einsum('fak,ftk->aft', left_corr[1], right_corr[1], precision=highest)
    imag_part = jnp.einsum('fak,ftk->aft', left_corr[1], right_corr[0], precision=highest) - jnp.einsum('fak,ftk->aft', left_corr[0], right_corr[1], precision=highest)
    return jnp.stack([real_part, imag_part], axis=1)

def reference(spectra, coda_bins, source_mask):
    white = whiten(spectra, coda_bins)
    all_ids = jnp.arange(NCH, dtype=jnp.int32)
    target_ids = all_ids[::STRIDE]
    targets = correlate(white[:, :, :, ::STRIDE], white) * mask_weights(source_mask, target_ids, all_ids)[None, None]
    block_rows = 256

    def one_block(block_index):
        first_row = (block_index * block_rows).astype(jnp.int32)
        left_white = lax.dynamic_slice_in_dim(white, first_row, block_rows, 3)
        row_ids = first_row + jnp.arange(block_rows, dtype=jnp.int32)
        masked = correlate(left_white, white) * mask_weights(source_mask, row_ids, all_ids)[None, None]
        return third(masked, targets)
    blocks = lax.map(one_block, jnp.arange(NCH // block_rows, dtype=jnp.int32))
    return blocks.reshape((NCH,) + blocks.shape[2:])
```

```python
import functools

import jax
import jax.numpy as jnp
from jax import lax
from jax.experimental import pallas as pl
from jax.experimental.pallas import tpu as pltpu
from jax.sharding import PartitionSpec as P

NTGT = 128
NT_DIMS = (((1,), (1,)), ((), ()))


def whiten_kernel(bins, spectra, *refs):
    count = (len(refs) - 2) // 1
    outs, held, sems = refs[:count], refs[count], refs[count + 1]
    copies = [
        pltpu.make_async_copy(spectra.at[:, bins[slot]], held.at[slot], sems.at[slot])
        for slot in range(count)
    ]
    for copy in copies:
        copy.start()
    for slot in range(count):
        copies[slot].wait()
        real, imag = held[slot, 0], held[slot, 1]
        power = jnp.mean(real * real + imag * imag, axis=1, keepdims=True)
        scale = 1.0 / jnp.sqrt(power + 1e-06)
        outs[slot][...] = jnp.concatenate([real * scale, imag * scale], axis=1).astype(jnp.bfloat16)


def whiten(spectra, bins):
    _, _, own, windows = spectra.shape
    count = bins.shape[0]
    return pl.pallas_call(
        whiten_kernel,
        grid_spec=pltpu.PrefetchScalarGridSpec(
            num_scalar_prefetch=1,
            grid=(1,),
            in_specs=[pl.BlockSpec(memory_space=pl.ANY)],
            out_specs=[pl.BlockSpec((own, 2 * windows), lambda s, b: (0, 0))] * count,
            scratch_shapes=[
                pltpu.VMEM((count, 2, own, windows), jnp.float32),
                pltpu.SemaphoreType.DMA((count,)),
            ],
        ),
        out_shape=[jax.ShapeDtypeStruct((own, 2 * windows), jnp.bfloat16)] * count,
        name="whiten",
    )(bins, spectra)


def quarter_turn(rows):
    half = rows.shape[1] // 2
    return jnp.concatenate([rows[:, half:], -rows[:, :half]], axis=1)


def third_kernel(layout, *refs):
    count, spread, own, spacing, grp = layout
    blocks = refs[: count * spread]
    kid, igrp, mask = refs[count * spread : count * spread + 3]
    outs = refs[count * spread + 3 : count * spread + 3 + count]
    everyone, turned, tmask, targets, acc = refs[count * spread + 3 + count :]
    f32, bf16 = jnp.float32, jnp.bfloat16
    chunk = spread * own
    groups = mask.shape[0]
    for at in range(count * spread):
        everyone[pl.ds(at * own, own), :] = blocks[at][...]
    for slot in range(count):
        turned[pl.ds(slot * own, own), :] = quarter_turn(blocks[slot * spread][...])
    table = mask[...].astype(f32).astype(bf16)
    tgroup = (lax.broadcasted_iota(jnp.int32, (groups, 2 * NTGT), 1) % NTGT) * spacing // grp
    lanes = (tgroup == lax.broadcasted_iota(jnp.int32, tgroup.shape, 0)).astype(f32).astype(bf16)
    tmask[...] = lax.dot_general(table, lanes, (((0,), (0,)), ((), ())), preferred_element_type=f32)
    rowpick = (igrp[...] == lax.broadcasted_iota(jnp.int32, (igrp.shape[0], groups), 1)).astype(f32).astype(bf16)
    rowmask = jnp.dot(rowpick, table, preferred_element_type=f32).astype(bf16)

    def pick(step, total):
        start = pl.multiple_of(step * chunk, chunk)
        ids = kid[pl.ds(step, 1), :]
        wanted = lax.broadcasted_iota(jnp.int32, (NTGT, chunk), 0) * spacing
        onehot = (ids == wanted).astype(f32).astype(bf16)
        return total + jnp.dot(onehot, everyone[pl.ds(start, chunk), :], preferred_element_type=f32)

    tgt = lax.fori_loop(0, count, pick, jnp.zeros((NTGT, everyone.shape[1]), f32)).astype(bf16)
    tturn = quarter_turn(tgt)
    targets[0] = jnp.concatenate([tgt, -tturn], axis=0)
    targets[1] = jnp.concatenate([tturn, tgt], axis=0)
    acc[...] = jnp.zeros_like(acc)

    def step_body(step, carry):
        start = pl.multiple_of(step * chunk, chunk)
        right = everyone[pl.ds(start, chunk), :]
        ids = kid[pl.ds(step, 1), :]
        colpick = (
            lax.broadcasted_iota(jnp.int32, (groups, chunk), 0) == ids // grp
        ).astype(f32)
        rows = jnp.dot(rowpick_mask(), colpick.astype(bf16), preferred_element_type=f32)
        tm = lax.dot_general(
            colpick.astype(bf16), tmask[...].astype(bf16), (((0,), (0,)), ((), ())), preferred_element_type=f32
        )
        r1 = (lax.dot_general(right, targets[0], NT_DIMS, preferred_element_type=f32) * tm).astype(bf16)
        r2 = (lax.dot_general(right, targets[1], NT_DIMS, preferred_element_type=f32) * tm).astype(bf16)
        for slot in range(count):
            at = pl.ds(slot * own, own)
            per = own // grp
            weight = jnp.broadcast_to(
                rows[slot * per : (slot + 1) * per][:, None, :], (per, grp, chunk)
            ).reshape(own, chunk)
            left = blocks[slot * spread][...]
            real = (lax.dot_general(left, right, NT_DIMS, preferred_element_type=f32) * weight).astype(bf16)
            imag = (lax.dot_general(turned[at, :], right, NT_DIMS, preferred_element_type=f32) * weight).astype(bf16)
            acc[at, :] += jnp.dot(real, r1, preferred_element_type=f32) + jnp.dot(
                imag, r2, preferred_element_type=f32
            )
        return carry

    def rowpick_mask():
        return rowmask

    lax.fori_loop(0, count, step_body, 0)
    windows = everyone.shape[1] // 2
    for slot in range(count):
        outs[slot][...] = (acc[pl.ds(slot * own, own), :] * (1.0 / (windows * windows))).astype(bf16)


def third(blocks, kid, igrp, mask, layout):
    count, spread, own, spacing, grp = layout
    width = blocks[0].shape[1]
    f32, bf16 = jnp.float32, jnp.bfloat16
    vmem = pl.BlockSpec(memory_space=pltpu.VMEM)
    return pl.pallas_call(
        functools.partial(third_kernel, layout),
        in_specs=[vmem] * (len(blocks) + 3),
        out_specs=[vmem] * count,
        out_shape=[jax.ShapeDtypeStruct((own, 2 * NTGT), bf16)] * count,
        scratch_shapes=[
            pltpu.VMEM((count * spread * own, width), bf16),
            pltpu.VMEM((count * own, width), bf16),
            pltpu.VMEM((mask.shape[0], 2 * NTGT), f32),
            pltpu.VMEM((2, 2 * NTGT, width), bf16),
            pltpu.VMEM((count * own, 2 * NTGT), f32),
        ],
        name="third",
    )(*blocks, kid, igrp, mask)


def finish_kernel(place, *refs):
    blocks, out = refs[:-1], refs[-1]
    count = len(blocks)
    own = blocks[0].shape[0]
    for slot, block in enumerate(blocks):
        value = block[...].astype(jnp.float32)
        for part in range(2):
            out[pl.ds(part * count + place[slot], own, stride=2 * count), :] = value[
                :, part * NTGT : (part + 1) * NTGT
            ]


def finish(blocks, place):
    own = blocks[0].shape[0]
    count = len(blocks)
    vmem = pl.BlockSpec(memory_space=pltpu.VMEM)
    out = pl.pallas_call(
        finish_kernel,
        in_specs=[pl.BlockSpec(memory_space=pltpu.SMEM)] + [vmem] * count,
        out_specs=vmem,
        out_shape=jax.ShapeDtypeStruct((own * 2 * count, NTGT), jnp.float32),
        name="finish",
    )(place, *blocks)
    return out.reshape(own, 2, count, NTGT)


def on_device(rows, spectra, coda_bins, source_mask):
    count = coda_bins.shape[0]
    spread = rows // count
    own = spectra.shape[2]
    channels = own * rows
    spacing = channels // NTGT
    grp = channels // source_mask.shape[0]
    me = lax.axis_index("row").astype(jnp.int32)
    mine, seat = me // spread, me % spread

    def swap(value, bits):
        return lax.ppermute(value, "row", [(r, r ^ bits) for r in range(rows)])

    slots = jnp.arange(count, dtype=jnp.int32)
    place = mine ^ slots
    white = whiten(spectra, coda_bins[place])
    blocks = [[white[0]] + [None] * (spread - 1)]
    for slot in range(1, count):
        blocks.append([swap(white[slot], slot * spread)] + [None] * (spread - 1))
    bit = spread // 2
    while bit >= 1:
        for slot in range(count):
            for held in range(0, spread, 2 * bit):
                blocks[slot][held + bit] = swap(blocks[slot][held], bit)
        bit //= 2
    seats = seat ^ jnp.arange(spread, dtype=jnp.int32)
    source = place[:, None] * spread + seats[None, :]
    kid = (source[:, :, None] * own + jnp.arange(own, dtype=jnp.int32)).reshape(count, spread * own)
    per = own // grp
    igrp = (((place * spread + seat) * per)[:, None] + jnp.arange(per, dtype=jnp.int32)).reshape(-1, 1)
    flat = [blocks[slot][held] for slot in range(count) for held in range(spread)]
    parts = third(flat, kid, igrp, source_mask, (count, spread, own, spacing, grp))
    back = [parts[0]] + [swap(parts[slot], slot * spread) for slot in range(1, count)]
    return finish(back, place)


def solution(mesh):
    return jax.shard_map(
        functools.partial(on_device, mesh.shape["row"]),
        mesh=mesh,
        in_specs=(P(None, None, "row", "band"), P("band"), P("band", None)),
        out_specs=P(("band", "row"), None, None, None),
        check_vma=False,
    )
```

```python
import functools

import jax
import jax.numpy as jnp
from jax import lax
from jax.experimental import pallas as pl
from jax.experimental.pallas import tpu as pltpu
from jax.sharding import PartitionSpec as P

NTGT = 128
NT_DIMS = (((1,), (1,)), ((), ()))
F32, BF16 = jnp.float32, jnp.bfloat16
VMEM = pl.BlockSpec(memory_space=pltpu.VMEM)
SMEM = pl.BlockSpec(memory_space=pltpu.SMEM)
ANY = pl.BlockSpec(memory_space=pl.ANY)


def whiten_kernel(spread, bins, spectra, *refs):
    count = len(refs) - 2
    outs, held, sems = refs[:count], refs[count], refs[count + 1]
    mine = lax.axis_index("row") // spread
    copies = [
        pltpu.make_async_copy(spectra.at[:, bins[mine ^ slot]], held.at[slot], sems.at[slot])
        for slot in range(count)
    ]
    for copy in copies:
        copy.start()
    for slot in range(count):
        copies[slot].wait()
        real, imag = held[slot, 0], held[slot, 1]
        power = jnp.mean(real * real + imag * imag, axis=1, keepdims=True)
        scale = 1.0 / jnp.sqrt(power + 1e-06)
        outs[slot][...] = jnp.concatenate([real * scale, imag * scale], axis=1).astype(BF16)


def whiten(spectra, bins, spread):
    _, _, own, windows = spectra.shape
    count = bins.shape[0]
    return pl.pallas_call(
        functools.partial(whiten_kernel, spread),
        in_specs=[SMEM, ANY],
        out_specs=[VMEM] * count,
        out_shape=[jax.ShapeDtypeStruct((own, 2 * windows), BF16)] * count,
        scratch_shapes=[
            pltpu.VMEM((count, 2, own, windows), F32),
            pltpu.SemaphoreType.DMA((count,)),
        ],
        name="whiten",
    )(bins, spectra)


def quarter_turn(rows):
    half = rows.shape[1] // 2
    return jnp.concatenate([rows[:, half:], -rows[:, :half]], axis=1)


def source_row(spread, slot, held):
    me = lax.axis_index("row")
    return ((me // spread) ^ slot) * spread + ((me % spread) ^ held)


def plan_kernel(layout, mask_s, mask_v, after, weights, subset):
    count, spread, own, spacing, grp = layout
    per = own // grp
    groups = mask_v.shape[0]
    table = mask_v[...].astype(F32).astype(BF16)
    rowg = (lax.broadcasted_iota(jnp.int32, (2 * NTGT, groups), 0) % NTGT) * spacing // grp
    rowpick = (rowg == lax.broadcasted_iota(jnp.int32, rowg.shape, 1)).astype(F32).astype(BF16)
    by_target = jnp.dot(rowpick, table, preferred_element_type=F32).astype(BF16)

    def block_body(at, carry):
        first_group = source_row(spread, at // spread, at % spread) * per
        lanes = first_group + lax.broadcasted_iota(jnp.int32, (groups, own), 1) // grp
        onehot = (lanes == lax.broadcasted_iota(jnp.int32, (groups, own), 0)).astype(F32).astype(BF16)
        weights[at] = jnp.dot(by_target, onehot, preferred_element_type=F32).astype(BF16)
        for slot in range(count):
            for part in range(per):
                group = source_row(spread, slot, 0) * per + part
                bits = mask_s[group, first_group]
                for b in range(1, per):
                    bits = bits + mask_s[group, first_group + b] * (1 << b)
                subset[at, slot * per + part] = bits
        return carry

    lax.fori_loop(0, count * spread, block_body, 0)


def plan(mask, after, layout):
    count, spread, own, spacing, grp = layout
    return pl.pallas_call(
        functools.partial(plan_kernel, layout),
        in_specs=[SMEM, VMEM, ANY],
        out_specs=[VMEM, SMEM],
        out_shape=[
            jax.ShapeDtypeStruct((count * spread, 2 * NTGT, own), BF16),
            jax.ShapeDtypeStruct((count * spread, count * own // grp), jnp.int32),
        ],
        name="plan",
    )(mask, mask, after)


def third_kernel(layout, subset, weights, *refs):
    count, spread, own, spacing, grp = layout
    blocks = refs[: count * spread]
    outs = refs[count * spread : count * spread + count]
    everyone, trows, both, tables, moved = refs[count * spread + count :]
    per, width, tper = own // grp, everyone.shape[-1], own // spacing
    half = width // 2
    for held in range(spread):
        for slot in range(count):
            block = blocks[slot * spread + held]
            everyone[held * count + slot] = block[...]
            row = source_row(spread, slot, held)
            for j in range(tper):
                trows[pl.ds(row * tper + j, 1), :] = block[pl.ds(j * spacing, 1), :].astype(F32)
    targets = trows[...].astype(BF16)
    both[0:NTGT] = targets
    both[NTGT:] = quarter_turn(targets)
    moved[...] = jnp.zeros_like(moved)
    for slot in range(count):
        tables[slot, 0] = jnp.zeros(tables.shape[2:], F32)
    lane = lax.broadcasted_iota(jnp.int32, (1, own), 1) // grp
    only = [jnp.where(lane == part, 1.0, 0.0).astype(BF16) for part in range(per)]

    def held_body(held, carry):
        for slot in range(count):
            block = everyone[held * count + slot]
            at = slot * spread + held
            corr = lax.dot_general(both[...], block, NT_DIMS, preferred_element_type=F32)
            corr = corr.astype(BF16) * weights[at]
            for part in range(per):
                v = jnp.dot(corr * only[part], block, preferred_element_type=F32)
                real = v[:NTGT, :half] - v[NTGT:, half:]
                imag = -(v[NTGT:, :half] + v[:NTGT, half:])
                one = jnp.concatenate([real, imag], axis=1)
                tables[slot, 1 << part] = one
                for low in range(1, 1 << part):
                    tables[slot, (1 << part) + low] = tables[slot, low] + one
        for group in range(count * per):
            total = tables[0, subset[held, group]]
            for slot in range(1, count):
                total = total + tables[slot, subset[slot * spread + held, group]]
            moved[group] += total
        return carry

    lax.fori_loop(0, spread, held_body, 0)
    for slot in range(count):
        left = blocks[slot * spread][...]
        for part in range(per):
            u = moved[slot * per + part]
            real, imag = u[:, :half], u[:, half:]
            right = jnp.concatenate(
                [jnp.concatenate([real, -imag], axis=1), jnp.concatenate([imag, real], axis=1)], axis=0
            ).astype(BF16)
            result = lax.dot_general(
                left[part * grp : (part + 1) * grp], right, NT_DIMS, preferred_element_type=F32
            )
            outs[slot][pl.ds(part * grp, grp), :] = (result * (1.0 / (half * half))).astype(BF16)


def third(blocks, subset, weights, layout):
    count, spread, own, spacing, grp = layout
    width = blocks[0].shape[-1]
    per = own // grp
    return pl.pallas_call(
        functools.partial(third_kernel, layout),
        in_specs=[SMEM, VMEM] + [VMEM] * (count * spread),
        out_specs=[VMEM] * count,
        out_shape=[jax.ShapeDtypeStruct((own, 2 * NTGT), BF16)] * count,
        scratch_shapes=[
            pltpu.VMEM((spread * count, own, width), BF16),
            pltpu.VMEM((NTGT, width), F32),
            pltpu.VMEM((2 * NTGT, width), BF16),
            pltpu.VMEM((count, 1 << per, NTGT, width), F32),
            pltpu.VMEM((count * per, NTGT, width), F32),
        ],
        name="third",
    )(subset, weights, *blocks)


def finish_kernel(spread, *refs):
    blocks, out = refs[:-1], refs[-1]
    count = len(blocks)
    own = blocks[0].shape[0]
    mine = lax.axis_index("row") // spread
    for slot, block in enumerate(blocks):
        value = block[...].astype(F32)
        for part in range(2):
            out[pl.ds(part * count + (mine ^ slot), own, stride=2 * count), :] = value[
                :, part * NTGT : (part + 1) * NTGT
            ]


def finish(blocks, spread):
    own = blocks[0].shape[0]
    count = len(blocks)
    out = pl.pallas_call(
        functools.partial(finish_kernel, spread),
        in_specs=[VMEM] * count,
        out_specs=VMEM,
        out_shape=jax.ShapeDtypeStruct((own * 2 * count, NTGT), F32),
        name="finish",
    )(*blocks)
    return out.reshape(own, 2, count, NTGT)


def on_device(rows, spectra, coda_bins, source_mask):
    count = coda_bins.shape[0]
    spread = rows // count
    own = spectra.shape[2]
    channels = own * rows
    layout = (count, spread, own, channels // NTGT, channels // source_mask.shape[0])

    def swap(value, bits):
        return lax.ppermute(value, "row", [(r, r ^ bits) for r in range(rows)])

    white = whiten(spectra, coda_bins, spread)
    weights, subset = plan(source_mask, white[0], layout)
    blocks = [[white[0]] + [None] * (spread - 1)]
    for slot in range(1, count):
        blocks.append([swap(white[slot], slot * spread)] + [None] * (spread - 1))
    bit = spread // 2
    while bit >= 1:
        for slot in range(count):
            for held in range(0, spread, 2 * bit):
                blocks[slot][held + bit] = swap(blocks[slot][held], bit)
        bit //= 2
    flat = [blocks[slot][held] for slot in range(count) for held in range(spread)]
    parts = third(flat, subset, weights, layout)
    back = [parts[0]] + [swap(parts[slot], slot * spread) for slot in range(1, count)]
    return finish(back, spread)


def solution(mesh):
    return jax.shard_map(
        functools.partial(on_device, mesh.shape["row"]),
        mesh=mesh,
        in_specs=(P(None, None, "row", "band"), P("band"), P("band", None)),
        out_specs=P(("band", "row"), None, None, None),
        check_vma=False,
    )
```

```python
import functools

import jax
import jax.numpy as jnp
from jax import lax
from jax.experimental import pallas as pl
from jax.experimental.pallas import tpu as pltpu
from jax.sharding import PartitionSpec as P

NTGT = 128
NT_DIMS = (((1,), (1,)), ((), ()))
F32, BF16 = jnp.float32, jnp.bfloat16
VMEM = pl.BlockSpec(memory_space=pltpu.VMEM)
SMEM = pl.BlockSpec(memory_space=pltpu.SMEM)
ANY = pl.BlockSpec(memory_space=pl.ANY)


def whiten_kernel(spread, bins, spectra, *refs):
    count = len(refs) - 2
    outs, held, sems = refs[:count], refs[count], refs[count + 1]
    mine = lax.axis_index("row") // spread
    copies = [
        pltpu.make_async_copy(spectra.at[:, bins[mine ^ slot]], held.at[slot], sems.at[slot])
        for slot in range(count)
    ]
    for copy in copies:
        copy.start()
    for slot in range(count):
        copies[slot].wait()
        real, imag = held[slot, 0], held[slot, 1]
        power = jnp.mean(real * real + imag * imag, axis=1, keepdims=True)
        scale = 1.0 / jnp.sqrt(power + 1e-06)
        outs[slot][...] = jnp.concatenate([real * scale, imag * scale], axis=1).astype(BF16)


def whiten(spectra, bins, spread):
    _, _, own, windows = spectra.shape
    count = bins.shape[0]
    return pl.pallas_call(
        functools.partial(whiten_kernel, spread),
        in_specs=[SMEM, ANY],
        out_specs=[VMEM] * count,
        out_shape=[pltpu.VMEM((own, 2 * windows), BF16)] * count,
        scratch_shapes=[
            pltpu.VMEM((count, 2, own, windows), F32),
            pltpu.SemaphoreType.DMA((count,)),
        ],
        name="whiten",
    )(bins, spectra)


def quarter_turn(rows):
    half = rows.shape[1] // 2
    return jnp.concatenate([rows[:, half:], -rows[:, :half]], axis=1)


def source_row(spread, slot, held):
    me = lax.axis_index("row")
    return ((me // spread) ^ slot) * spread + ((me % spread) ^ held)


def third_kernel(layout, mask_s, mask_v, *refs):
    count, spread, own, spacing, grp = layout
    blocks = refs[: count * spread]
    outs = refs[count * spread : count * spread + count]
    everyone, trows, both, wanted, tables, moved = refs[count * spread + count :]
    per, width, tper = own // grp, everyone.shape[-1], own // spacing
    half, groups, tile = width // 2, mask_v.shape[0], 16
    rowg = (lax.broadcasted_iota(jnp.int32, (2 * NTGT, groups), 0) % NTGT) * spacing // grp
    rowpick = (rowg == lax.broadcasted_iota(jnp.int32, rowg.shape, 1)).astype(F32).astype(BF16)
    wanted[...] = jnp.dot(
        rowpick, mask_v[...].astype(F32).astype(BF16), preferred_element_type=F32
    ).astype(BF16)
    for held in range(spread):
        for slot in range(count):
            block = blocks[slot * spread + held]
            everyone[held * count + slot] = block[...]
            row = source_row(spread, slot, held)
            for j in range(tper):
                trows[pl.ds(row * tper + j, 1), :] = block[pl.ds(j * spacing, 1), :].astype(F32)
    targets = trows[...].astype(BF16)
    both[0:NTGT] = targets
    both[NTGT:] = quarter_turn(targets)
    moved[...] = jnp.zeros_like(moved)
    for slot in range(count):
        tables[slot, 0] = jnp.zeros(tables.shape[2:], F32)
    lane = lax.broadcasted_iota(jnp.int32, (1, own), 1) // grp
    only = [jnp.where(lane == part, 1.0, 0.0).astype(BF16) for part in range(per)]
    group_rows = lax.broadcasted_iota(jnp.int32, (groups, own), 0)
    group_lanes = lax.broadcasted_iota(jnp.int32, (groups, own), 1) // grp

    def held_body(held, carry):
        for slot in range(count):
            block = everyone[held * count + slot]
            first_group = source_row(spread, slot, held) * per
            onehot = (group_rows == first_group + group_lanes).astype(F32).astype(BF16)
            weight = jnp.dot(wanted[...], onehot, preferred_element_type=F32)
            corr = lax.dot_general(both[...], block, NT_DIMS, preferred_element_type=F32)
            corr = (corr * weight).astype(BF16)
            parts = [corr * only[part] for part in range(per)]
            left = jnp.concatenate(
                [
                    piece
                    for t in range(0, NTGT, tile)
                    for part in parts
                    for piece in (part[t : t + tile], part[NTGT + t : NTGT + t + tile])
                ],
                axis=0,
            )
            v = jnp.dot(left, block, preferred_element_type=F32)
            for t in range(0, NTGT, tile):
                sums = [None]
                for part in range(per):
                    at = (t * per + part * tile) * 2
                    vr, vi = v[at : at + tile], v[at + tile : at + 2 * tile]
                    one = jnp.concatenate(
                        [vr[:, :half] - vi[:, half:], -(vi[:, :half] + vr[:, half:])], axis=1
                    )
                    sums += [one] + [low + one for low in sums[1:]]
                for pick in range(1, len(sums)):
                    tables[slot, pick, t : t + tile] = sums[pick]
        for group in range(count * per):
            receiver = source_row(spread, group // per, 0) * per + group % per
            total = moved[group]
            for slot in range(count):
                first_group = source_row(spread, slot, held) * per
                bits = mask_s[receiver, first_group]
                for b in range(1, per):
                    bits = bits + mask_s[receiver, first_group + b] * (1 << b)
                total = total + tables[slot, bits]
            moved[group] = total
        return carry

    lax.fori_loop(0, spread, held_body, 0)
    for slot in range(count):
        left = blocks[slot * spread][...]
        for part in range(per):
            u = moved[slot * per + part]
            real, imag = u[:, :half], u[:, half:]
            right = jnp.concatenate(
                [jnp.concatenate([real, -imag], axis=1), jnp.concatenate([imag, real], axis=1)], axis=0
            ).astype(BF16)
            result = lax.dot_general(
                left[part * grp : (part + 1) * grp], right, NT_DIMS, preferred_element_type=F32
            )
            outs[slot][pl.ds(part * grp, grp), :] = (result * (1.0 / (half * half))).astype(BF16)


def near(value):
    return pltpu.with_memory_space_constraint(value, pltpu.VMEM)


def third(blocks, mask, layout):
    count, spread, own, spacing, grp = layout
    width = blocks[0].shape[-1]
    per = own // grp
    return pl.pallas_call(
        functools.partial(third_kernel, layout),
        in_specs=[SMEM, VMEM] + [VMEM] * (count * spread),
        out_specs=[VMEM] * count,
        out_shape=[pltpu.VMEM((own, 2 * NTGT), BF16)] * count,
        scratch_shapes=[
            pltpu.VMEM((spread * count, own, width), BF16),
            pltpu.VMEM((NTGT, width), F32),
            pltpu.VMEM((2 * NTGT, width), BF16),
            pltpu.VMEM((2 * NTGT, mask.shape[0]), BF16),
            pltpu.VMEM((count, 1 << per, NTGT, width), F32),
            pltpu.VMEM((count * per, NTGT, width), F32),
        ],
        name="third",
    )(mask, mask, *map(near, blocks))


def finish_kernel(spread, *refs):
    blocks, out = refs[:-1], refs[-1]
    count = len(blocks)
    own = blocks[0].shape[0]
    mine = lax.axis_index("row") // spread
    for slot, block in enumerate(blocks):
        value = block[...].astype(F32)
        for part in range(2):
            out[pl.ds(part * count + (mine ^ slot), own, stride=2 * count), :] = value[
                :, part * NTGT : (part + 1) * NTGT
            ]


def finish(blocks, spread):
    own = blocks[0].shape[0]
    count = len(blocks)
    out = pl.pallas_call(
        functools.partial(finish_kernel, spread),
        in_specs=[VMEM] * count,
        out_specs=VMEM,
        out_shape=jax.ShapeDtypeStruct((own * 2 * count, NTGT), F32),
        name="finish",
    )(*map(near, blocks))
    return out.reshape(own, 2, count, NTGT)


def on_device(rows, spectra, coda_bins, source_mask):
    count = coda_bins.shape[0]
    spread = rows // count
    own = spectra.shape[2]
    channels = own * rows
    layout = (count, spread, own, channels // NTGT, channels // source_mask.shape[0])

    def swap(value, bits):
        return lax.ppermute(value, "row", [(r, r ^ bits) for r in range(rows)])

    white = whiten(spectra, coda_bins, spread)
    blocks = [[white[0]] + [None] * (spread - 1)]
    for slot in range(1, count):
        blocks.append([swap(white[slot], slot * spread)] + [None] * (spread - 1))
    bit = spread // 2
    while bit >= 1:
        for slot in range(count):
            for held in range(0, spread, 2 * bit):
                blocks[slot][held + bit] = swap(blocks[slot][held], bit)
        bit //= 2
    flat = [blocks[slot][held] for slot in range(count) for held in range(spread)]
    parts = third(flat, source_mask, layout)
    back = [parts[0]] + [swap(parts[slot], slot * spread) for slot in range(1, count)]
    return finish(back, spread)


def solution(mesh):
    return jax.shard_map(
        functools.partial(on_device, mesh.shape["row"]),
        mesh=mesh,
        in_specs=(P(None, None, "row", "band"), P("band"), P("band", None)),
        out_specs=P(("band", "row"), None, None, None),
        check_vma=False,
    )
```

```python
import functools

import jax
import jax.numpy as jnp
from jax import lax
from jax.experimental import pallas as pl
from jax.experimental.pallas import tpu as pltpu
from jax.sharding import PartitionSpec as P


NTGT = 128
NT_DIMS = (((1,), (1,)), ((), ()))
F32, BF16 = jnp.float32, jnp.bfloat16
VMEM = pl.BlockSpec(memory_space=pltpu.VMEM)
SMEM = pl.BlockSpec(memory_space=pltpu.SMEM)
ANY = pl.BlockSpec(memory_space=pl.ANY)


def ready(layout, mask, packed, wanted):
    _, _, own, spacing, grp = layout
    per, groups = own // grp, mask.shape[0]
    values = mask[...].astype(F32).astype(BF16)
    group = lax.broadcasted_iota(jnp.int32, (groups, 128), 0)
    column = lax.broadcasted_iota(jnp.int32, (groups, 128), 1)
    bit = lax.shift_left(jnp.int32(1), group & (per - 1))
    here = lax.shift_right_logical(group, per.bit_length() - 1) == column
    weight = jnp.where(here, bit, 0).astype(F32).astype(BF16)
    packed[...] = jnp.dot(values, weight, preferred_element_type=F32).astype(jnp.int32)
    rows_of = lax.broadcasted_iota(jnp.int32, (NTGT, groups), 0)
    rowg = lax.shift_right_logical(rows_of, (grp // spacing).bit_length() - 1)
    rowpick = (rowg == lax.broadcasted_iota(jnp.int32, rowg.shape, 1)).astype(F32).astype(BF16)
    values = jnp.concatenate([values, jnp.zeros((groups, 128), BF16)], axis=1)[:, :128]
    wanted[...] = jnp.dot(rowpick, values, preferred_element_type=F32)


def whiten_kernel(layout, bins, spectra, mask, *refs):
    count, spread = layout[:2]
    outs, (packed, wanted, held, sems, near_mask, mask_sem) = refs[:count], refs[count:]
    mine = lax.axis_index("row") // spread
    fetch = pltpu.make_async_copy(mask, near_mask, mask_sem)
    copies = [
        pltpu.make_async_copy(spectra.at[:, bins[mine ^ slot]], held.at[slot], sems.at[slot])
        for slot in range(count)
    ]
    for copy in (*copies, fetch):
        copy.start()
    for slot in range(count):
        copies[slot].wait()
        real, imag = held[slot, 0], held[slot, 1]
        power = jnp.mean(real * real + imag * imag, axis=1, keepdims=True)
        scale = 1.0 / jnp.sqrt(power + 1e-06)
        outs[slot][...] = jnp.concatenate([real * scale, imag * scale], axis=1).astype(BF16)
    fetch.wait()
    ready(layout, near_mask, packed, wanted)


def whiten(spectra, bins, mask, layout):
    _, _, own, windows = spectra.shape
    count = bins.shape[0]
    return pl.pallas_call(
        functools.partial(whiten_kernel, layout),
        in_specs=[SMEM, ANY, ANY],
        out_specs=[VMEM] * (count + 2),
        out_shape=[pltpu.VMEM((own, 2 * windows), BF16)] * count
        + [pltpu.VMEM((mask.shape[0], 128), jnp.int32), pltpu.VMEM((NTGT, 128), F32)],
        scratch_shapes=[
            pltpu.VMEM((count, 2, own, windows), F32),
            pltpu.SemaphoreType.DMA((count,)),
            pltpu.VMEM(mask.shape, jnp.int32),
            pltpu.SemaphoreType.DMA,
        ],
        name="whiten",
    )(bins, spectra, mask)


def quarter_turn(rows):
    half = rows.shape[1] // 2
    return jnp.concatenate([-rows[:, half:], rows[:, :half]], axis=1)


def source_row(spread, slot, held):
    me = lax.axis_index("row")
    return ((me // spread) ^ slot) * spread + ((me % spread) ^ held)


def table_place(layout, slot, held):
    count, _, own, _, grp = layout
    part = count // 2
    return slot // part, (held * part + slot % part) * (1 << (own // grp))


def receive(layout, slots, tables, table, right, lefts, outs):
    count, spread, own, _, grp = layout
    per, width = own // grp, right.shape[-1]
    half = width // 2

    def receiver_body(at, carry):
        slot = slots[0] + lax.shift_right_logical(at, per.bit_length() - 1)
        receiver = source_row(spread, slot, 0) * per + (at & (per - 1))
        total = None
        for held in range(spread):
            for piece in range(count):
                bits = table[receiver, source_row(spread, piece, held)]
                which, base = table_place(layout, piece, held)
                term = tables[which][jnp.where(bits == 0, 0, bits + base)]
                total = term if total is None else total + term
        right[at, 0:NTGT] = total.astype(BF16)
        right[at, NTGT:] = quarter_turn(total).astype(BF16)
        return carry

    lax.fori_loop(0, len(slots) * per, receiver_body, 0)
    for at in range(len(slots)):
        for part in range(per):
            rows = pl.ds(part * grp, grp)
            result = lax.dot_general(
                lefts[at][rows, :], right[at * per + part], NT_DIMS, preferred_element_type=F32
            )
            outs[at][rows, :] = (result * (1.0 / (half * half))).astype(BF16)


def third_kernel(layout, slots, packed, wanted, *refs):
    count, spread, own, spacing, grp = layout
    blocks, refs = refs[: count * spread], refs[count * spread :]
    tables, refs = refs[:2], refs[2:]
    outs, refs = refs[: len(slots)], refs[len(slots) :]
    everyone, trows, targets, right, table, sem = refs
    copy = pltpu.make_async_copy(packed, table, sem)
    copy.start()
    per, tper = own // grp, own // spacing
    tile, duo = 16, min(2, own // grp)
    span = duo * grp
    for held in range(spread):
        for slot in range(count):
            block = blocks[slot * spread + held]
            everyone[held * count + slot] = block[...]
            row = source_row(spread, slot, held)
            for j in range(tper):
                trows[pl.ds(row * tper + j, 1), :] = block[pl.ds(j * spacing, 1), :].astype(F32)
    value = trows[...].astype(BF16)
    targets[0:NTGT] = value
    targets[NTGT:] = -quarter_turn(value)
    for one in tables:
        one[0] = jnp.zeros(one.shape[1:], F32)
    lane = lax.shift_right_logical(
        lax.broadcasted_iota(jnp.int32, (NTGT, 128), 1), grp.bit_length() - 1
    )

    def held_body(held, carry):
        for slot in range(count):
            which, base = table_place(layout, slot, held)
            at = held * count + slot
            first_group = source_row(spread, slot, held) * per
            block = everyone[at]
            turned = quarter_turn(block)
            corr = lax.dot_general(targets[...], block, NT_DIMS, preferred_element_type=F32)
            results = []
            for low in range(0, per, duo):
                lanes = slice(low * grp, low * grp + span)
                lefts = []
                for one in range(duo):
                    pickup = jnp.where(lane == one, first_group + low + one, 127)
                    weight = jnp.take_along_axis(wanted[...], pickup, axis=1)[:, :span]
                    lefts.append(
                        jnp.concatenate(
                            [corr[:NTGT, lanes] * weight, corr[NTGT:, lanes] * weight], axis=1
                        ).astype(BF16)
                    )
                left = jnp.concatenate(
                    [part[t : t + tile] for t in range(0, NTGT, tile) for part in lefts], axis=0
                )
                both = jnp.concatenate([block[lanes], turned[lanes]], axis=0)
                results.append(jnp.dot(left, both, preferred_element_type=F32))
            for t in range(0, NTGT, tile):
                sums = [None]
                for part in range(per):
                    row = t * duo + (part % duo) * tile
                    one = results[part // duo][row : row + tile]
                    sums += [one] + [low + one for low in sums[1:]]
                for subset in range(1, len(sums)):
                    tables[which][base + subset, t : t + tile] = sums[subset]
        return carry

    lax.fori_loop(0, spread, held_body, 0)
    copy.wait()
    lefts = [blocks[slot * spread] for slot in slots]
    receive(layout, slots, tables, table, right, lefts, outs)


def rest_kernel(layout, slots, packed, first, second, *refs):
    lefts, refs = refs[: len(slots)], refs[len(slots) :]
    outs, (right, table, sem) = refs[: len(slots)], refs[len(slots) :]
    copy = pltpu.make_async_copy(packed, table, sem)
    copy.start()
    copy.wait()
    receive(layout, slots, (first, second), table, right, lefts, outs)


def near(value):
    return pltpu.with_memory_space_constraint(value, pltpu.VMEM)


def scratch(layout, slots, groups, width):
    _, _, own, _, grp = layout
    return [
        pltpu.VMEM((len(slots) * own // grp, 2 * NTGT, width), BF16),
        pltpu.SMEM((groups, 128), jnp.int32),
        pltpu.SemaphoreType.DMA,
    ]


def third(blocks, slots, packed, wanted, layout):
    count, spread, own, _, grp = layout
    width, per = blocks[0].shape[-1], own // grp
    return pl.pallas_call(
        functools.partial(third_kernel, layout, slots),
        in_specs=[VMEM] * (2 + count * spread),
        out_specs=[VMEM] * (2 + len(slots)),
        out_shape=[pltpu.VMEM(((count * spread // 2) << per, NTGT, width), F32)] * 2
        + [pltpu.VMEM((own, 2 * NTGT), BF16)] * len(slots),
        scratch_shapes=[
            pltpu.VMEM((count * spread, own, width), BF16),
            pltpu.VMEM((NTGT, width), F32),
            pltpu.VMEM((2 * NTGT, width), BF16),
        ]
        + scratch(layout, slots, packed.shape[0], width),
        compiler_params=pltpu.CompilerParams(vmem_limit_bytes=12 << 20),
        name="third",
    )(near(packed), near(wanted), *map(near, blocks))


def rest(lefts, slots, packed, tables, layout):
    own, width = lefts[0].shape
    return pl.pallas_call(
        functools.partial(rest_kernel, layout, slots),
        in_specs=[VMEM] * (3 + len(slots)),
        out_specs=[VMEM] * len(slots),
        out_shape=[pltpu.VMEM((own, 2 * NTGT), BF16)] * len(slots),
        scratch_shapes=scratch(layout, slots, packed.shape[0], width),
        compiler_params=pltpu.CompilerParams(vmem_limit_bytes=12 << 20),
        name="rest",
    )(near(packed), *map(near, tables), *map(near, lefts))


def finish_kernel(spread, *refs):
    blocks, out = refs[:-1], refs[-1]
    count = len(blocks)
    own = blocks[0].shape[0]
    mine = lax.axis_index("row") // spread
    for slot, block in enumerate(blocks):
        value = block[...].astype(F32)
        for part in range(2):
            out[pl.ds(part * count + (mine ^ slot), own, stride=2 * count), :] = value[
                :, part * NTGT : (part + 1) * NTGT
            ]


def finish(blocks, spread):
    own = blocks[0].shape[0]
    count = len(blocks)
    out = pl.pallas_call(
        functools.partial(finish_kernel, spread),
        in_specs=[VMEM] * count,
        out_specs=VMEM,
        out_shape=jax.ShapeDtypeStruct((own * 2 * count, NTGT), F32),
        name="finish",
    )(*map(near, blocks))
    return out.reshape(own, 2, count, NTGT)


def on_device(rows, spectra, coda_bins, source_mask):
    count = coda_bins.shape[0]
    spread = rows // count
    own = spectra.shape[2]
    channels = own * rows
    layout = (count, spread, own, channels // NTGT, channels // source_mask.shape[0])

    def swap(value, bits):
        return lax.ppermute(value, "row", [(r, r ^ bits) for r in range(rows)])

    *white, packed, wanted = whiten(spectra, coda_bins, source_mask, layout)
    blocks = [[white[0]] + [None] * (spread - 1)]
    for slot in range(1, count):
        blocks.append([swap(white[slot], slot * spread)] + [None] * (spread - 1))
    bit = spread // 2
    while bit >= 1:
        for slot in range(count):
            for held in range(0, spread, 2 * bit):
                blocks[slot][held + bit] = swap(blocks[slot][held], bit)
        bit //= 2
    flat = [blocks[slot][held] for slot in range(count) for held in range(spread)]
    stages = [(slot,) for slot in range(count // 2, count)] + [tuple(range(count // 2))]
    first, second, *parts = third(flat, stages[0], packed, wanted, layout)
    results = dict(zip(stages[0], parts))
    for stage in stages[1:]:
        lefts = [blocks[slot][0] for slot in stage]
        results.update(zip(stage, rest(lefts, stage, packed, (first, second), layout)))
    back = [results[0]] + [swap(results[slot], slot * spread) for slot in range(1, count)]
    return finish(back, spread)


def solution(mesh):
    def body(spectra, coda_bins, source_mask):
        return on_device(mesh.shape["row"], spectra, coda_bins, source_mask)

    return jax.shard_map(
        body,
        mesh=mesh,
        in_specs=(P(None, None, "row", "band"), P("band"), P("band", None)),
        out_specs=P(("band", "row"), None, None, None),
        check_vma=False,
    )
```

```python
import functools

import jax
import jax.numpy as jnp
from jax import lax
from jax.experimental import pallas as pl
from jax.experimental.pallas import tpu as pltpu
from jax.sharding import PartitionSpec as P


NTGT = 128
NT_DIMS = (((1,), (1,)), ((), ()))
F32, BF16 = jnp.float32, jnp.bfloat16
VMEM = pl.BlockSpec(memory_space=pltpu.VMEM)
SMEM = pl.BlockSpec(memory_space=pltpu.SMEM)
ANY = pl.BlockSpec(memory_space=pl.ANY)


def ready(layout, mask, packed, wanted):
    _, _, own, spacing, grp = layout
    per, groups = own // grp, mask.shape[0]
    values = mask[...].astype(F32).astype(BF16)
    group = lax.broadcasted_iota(jnp.int32, (groups, 128), 0)
    column = lax.broadcasted_iota(jnp.int32, (groups, 128), 1)
    bit = lax.shift_left(jnp.int32(1), group & (per - 1))
    here = lax.shift_right_logical(group, per.bit_length() - 1) == column
    weight = jnp.where(here, bit, 0).astype(F32).astype(BF16)
    packed[...] = jnp.dot(values, weight, preferred_element_type=F32).astype(jnp.int32)
    rows_of = lax.broadcasted_iota(jnp.int32, (NTGT, groups), 0)
    rowg = lax.shift_right_logical(rows_of, (grp // spacing).bit_length() - 1)
    rowpick = (rowg == lax.broadcasted_iota(jnp.int32, rowg.shape, 1)).astype(F32).astype(BF16)
    values = jnp.concatenate([values, jnp.zeros((groups, 128), BF16)], axis=1)[:, :128]
    wanted[...] = jnp.dot(rowpick, values, preferred_element_type=F32)


def whiten_kernel(layout, slots, bins, spectra, mask, *refs):
    spread, final = layout[1], 0 in slots
    outs, refs = refs[: len(slots)], refs[len(slots) :]
    if final:
        packed, wanted, near_mask, mask_sem, *refs = refs
    held, sems = refs
    mine = lax.axis_index("row") // spread
    copies = [
        pltpu.make_async_copy(spectra.at[:, bins[mine ^ slot]], held.at[at], sems.at[at])
        for at, slot in enumerate(slots)
    ]
    if final:
        copies.append(pltpu.make_async_copy(mask, near_mask, mask_sem))
    for copy in copies:
        copy.start()
    for at in range(len(slots)):
        copies[at].wait()
        real, imag = held[at, 0], held[at, 1]
        power = jnp.mean(real * real + imag * imag, axis=1, keepdims=True)
        scale = 1.0 / jnp.sqrt(power + 1e-06)
        outs[at][...] = jnp.concatenate([real * scale, imag * scale], axis=1).astype(BF16)
    if final:
        copies[-1].wait()
        ready(layout, near_mask, packed, wanted)


def whiten(spectra, bins, mask, slots, layout):
    _, _, own, windows = spectra.shape
    final = 0 in slots
    tables = [pltpu.VMEM((mask.shape[0], 128), jnp.int32), pltpu.VMEM((NTGT, 128), F32)]
    fetched = [pltpu.VMEM(mask.shape, jnp.int32), pltpu.SemaphoreType.DMA]
    return pl.pallas_call(
        functools.partial(whiten_kernel, layout, slots),
        in_specs=[SMEM, ANY, ANY],
        out_specs=[VMEM] * (len(slots) + 2 * final),
        out_shape=[pltpu.VMEM((own, 2 * windows), BF16)] * len(slots) + tables * final,
        scratch_shapes=fetched * final
        + [
            pltpu.VMEM((len(slots), 2, own, windows), F32),
            pltpu.SemaphoreType.DMA((len(slots),)),
        ],
        name="whiten",
    )(bins, spectra, mask)


def quarter_turn(rows):
    half = rows.shape[1] // 2
    return jnp.concatenate([-rows[:, half:], rows[:, :half]], axis=1)


def source_row(spread, slot, held):
    me = lax.axis_index("row")
    return ((me // spread) ^ slot) * spread + ((me % spread) ^ held)


def table_place(layout, slot, held):
    count, _, own, _, grp = layout
    part = count // 2
    return slot // part, (held * part + slot % part) * (1 << (own // grp))


def receive(layout, slots, tables, table, right, lefts, outs):
    count, spread, own, _, grp = layout
    per, width = own // grp, right.shape[-1]
    half = width // 2

    def receiver_body(at, carry):
        slot = slots[0] + lax.shift_right_logical(at, per.bit_length() - 1)
        receiver = source_row(spread, slot, 0) * per + (at & (per - 1))
        total = None
        for held in range(spread):
            for piece in range(count):
                bits = table[receiver, source_row(spread, piece, held)]
                which, base = table_place(layout, piece, held)
                term = tables[which][jnp.where(bits == 0, 0, bits + base)]
                total = term if total is None else total + term
        right[at, 0:NTGT] = total.astype(BF16)
        right[at, NTGT:] = quarter_turn(total).astype(BF16)
        return carry

    lax.fori_loop(0, len(slots) * per, receiver_body, 0)
    for at in range(len(slots)):
        for part in range(per):
            rows = pl.ds(part * grp, grp)
            result = lax.dot_general(
                lefts[at][rows, :], right[at * per + part], NT_DIMS, preferred_element_type=F32
            )
            outs[at][rows, :] = (result * (1.0 / (half * half))).astype(BF16)


def third_kernel(layout, slots, packed, wanted, *refs):
    count, spread, own, spacing, grp = layout
    blocks, refs = refs[: count * spread], refs[count * spread :]
    tables, refs = refs[:2], refs[2:]
    outs, refs = refs[: len(slots)], refs[len(slots) :]
    everyone, trows, targets, right, table, sem = refs
    copy = pltpu.make_async_copy(packed, table, sem)
    copy.start()
    per, tper = own // grp, own // spacing
    tile, duo = 16, min(2, own // grp)
    span = duo * grp
    for held in range(spread):
        for slot in range(count):
            block = blocks[slot * spread + held]
            everyone[held * count + slot] = block[...]
            row = source_row(spread, slot, held)
            for j in range(tper):
                trows[pl.ds(row * tper + j, 1), :] = block[pl.ds(j * spacing, 1), :].astype(F32)
    value = trows[...].astype(BF16)
    targets[0:NTGT] = value
    targets[NTGT:] = -quarter_turn(value)
    for one in tables:
        one[0] = jnp.zeros(one.shape[1:], F32)
    lane = lax.shift_right_logical(
        lax.broadcasted_iota(jnp.int32, (NTGT, 128), 1), grp.bit_length() - 1
    )

    def held_body(held, carry):
        for slot in range(count):
            which, base = table_place(layout, slot, held)
            at = held * count + slot
            first_group = source_row(spread, slot, held) * per
            block = everyone[at]
            turned = quarter_turn(block)
            corr = lax.dot_general(targets[...], block, NT_DIMS, preferred_element_type=F32)
            results = []
            for low in range(0, per, duo):
                lanes = slice(low * grp, low * grp + span)
                lefts = []
                for one in range(duo):
                    pickup = jnp.where(lane == one, first_group + low + one, 127)
                    weight = jnp.take_along_axis(wanted[...], pickup, axis=1)[:, :span]
                    lefts.append(
                        jnp.concatenate(
                            [corr[:NTGT, lanes] * weight, corr[NTGT:, lanes] * weight], axis=1
                        ).astype(BF16)
                    )
                left = jnp.concatenate(
                    [part[t : t + tile] for t in range(0, NTGT, tile) for part in lefts], axis=0
                )
                both = jnp.concatenate([block[lanes], turned[lanes]], axis=0)
                results.append(jnp.dot(left, both, preferred_element_type=F32))
            for t in range(0, NTGT, tile):
                sums = [None]
                for part in range(per):
                    row = t * duo + (part % duo) * tile
                    one = results[part // duo][row : row + tile]
                    sums += [one] + [low + one for low in sums[1:]]
                for subset in range(1, len(sums)):
                    tables[which][base + subset, t : t + tile] = sums[subset]
        return carry

    lax.fori_loop(0, spread, held_body, 0)
    copy.wait()
    lefts = [blocks[slot * spread] for slot in slots]
    receive(layout, slots, tables, table, right, lefts, outs)


def rest_kernel(layout, slots, packed, first, second, *refs):
    lefts, refs = refs[: len(slots)], refs[len(slots) :]
    outs, (right, table, sem) = refs[: len(slots)], refs[len(slots) :]
    copy = pltpu.make_async_copy(packed, table, sem)
    copy.start()
    copy.wait()
    receive(layout, slots, (first, second), table, right, lefts, outs)


def near(value):
    return pltpu.with_memory_space_constraint(value, pltpu.VMEM)


def scratch(layout, slots, groups, width):
    _, _, own, _, grp = layout
    return [
        pltpu.VMEM((len(slots) * own // grp, 2 * NTGT, width), BF16),
        pltpu.SMEM((groups, 128), jnp.int32),
        pltpu.SemaphoreType.DMA,
    ]


def third(blocks, slots, packed, wanted, layout):
    count, spread, own, _, grp = layout
    width, per = blocks[0].shape[-1], own // grp
    return pl.pallas_call(
        functools.partial(third_kernel, layout, slots),
        in_specs=[VMEM] * (2 + count * spread),
        out_specs=[VMEM] * (2 + len(slots)),
        out_shape=[pltpu.VMEM(((count * spread // 2) << per, NTGT, width), F32)] * 2
        + [pltpu.VMEM((own, 2 * NTGT), BF16)] * len(slots),
        scratch_shapes=[
            pltpu.VMEM((count * spread, own, width), BF16),
            pltpu.VMEM((NTGT, width), F32),
            pltpu.VMEM((2 * NTGT, width), BF16),
        ]
        + scratch(layout, slots, packed.shape[0], width),
        compiler_params=pltpu.CompilerParams(vmem_limit_bytes=12 << 20),
        name="third",
    )(near(packed), near(wanted), *map(near, blocks))


def rest(lefts, slots, packed, tables, layout):
    own, width = lefts[0].shape
    return pl.pallas_call(
        functools.partial(rest_kernel, layout, slots),
        in_specs=[VMEM] * (3 + len(slots)),
        out_specs=[VMEM] * len(slots),
        out_shape=[pltpu.VMEM((own, 2 * NTGT), BF16)] * len(slots),
        scratch_shapes=scratch(layout, slots, packed.shape[0], width),
        compiler_params=pltpu.CompilerParams(vmem_limit_bytes=12 << 20),
        name="rest",
    )(near(packed), *map(near, tables), *map(near, lefts))


def finish_kernel(spread, *refs):
    blocks, out = refs[:-1], refs[-1]
    count = len(blocks)
    own = blocks[0].shape[0]
    mine = lax.axis_index("row") // spread
    for slot, block in enumerate(blocks):
        value = block[...].astype(F32)
        for part in range(2):
            out[pl.ds(part * count + (mine ^ slot), own, stride=2 * count), :] = value[
                :, part * NTGT : (part + 1) * NTGT
            ]


def finish(blocks, spread):
    own = blocks[0].shape[0]
    count = len(blocks)
    out = pl.pallas_call(
        functools.partial(finish_kernel, spread),
        in_specs=[VMEM] * count,
        out_specs=VMEM,
        out_shape=jax.ShapeDtypeStruct((own * 2 * count, NTGT), F32),
        name="finish",
    )(*map(near, blocks))
    return out.reshape(own, 2, count, NTGT)


def on_device(rows, spectra, coda_bins, source_mask):
    count = coda_bins.shape[0]
    spread = rows // count
    own = spectra.shape[2]
    channels = own * rows
    layout = (count, spread, own, channels // NTGT, channels // source_mask.shape[0])

    def swap(value, bits):
        return lax.ppermute(value, "row", [(r, r ^ bits) for r in range(rows)])

    first_slots = (1, 2)
    other = tuple(slot for slot in range(count) if slot not in first_slots)
    white = dict(zip(first_slots, whiten(spectra, coda_bins, source_mask, first_slots, layout)))
    *more, packed, wanted = whiten(spectra, coda_bins, source_mask, other, layout)
    white.update(zip(other, more))
    blocks = [[white[0]] + [None] * (spread - 1)]
    for slot in range(1, count):
        blocks.append([swap(white[slot], slot * spread)] + [None] * (spread - 1))
    bit = spread // 2
    while bit >= 1:
        for slot in range(count):
            for held in range(0, spread, 2 * bit):
                blocks[slot][held + bit] = swap(blocks[slot][held], bit)
        bit //= 2
    flat = [blocks[slot][held] for slot in range(count) for held in range(spread)]
    stages = [(slot,) for slot in range(count // 2, count)] + [tuple(range(count // 2))]
    first, second, *parts = third(flat, stages[0], packed, wanted, layout)
    results = dict(zip(stages[0], parts))
    for stage in stages[1:]:
        lefts = [blocks[slot][0] for slot in stage]
        results.update(zip(stage, rest(lefts, stage, packed, (first, second), layout)))
    back = [results[0]] + [swap(results[slot], slot * spread) for slot in range(1, count)]
    return finish(back, spread)


def solution(mesh):
    def body(spectra, coda_bins, source_mask):
        return on_device(mesh.shape["row"], spectra, coda_bins, source_mask)

    return jax.shard_map(
        body,
        mesh=mesh,
        in_specs=(P(None, None, "row", "band"), P("band"), P("band", None)),
        out_specs=P(("band", "row"), None, None, None),
        check_vma=False,
    )
```
